32 devices in a mesh: tm: 16 (over z, x, core), acct: 2 (over y).
Axes of the slice: x: 2, y: 2, z: 4, core: 2. Of those that a mesh axis runs over, the one named last changes fastest.
Arguments:
- returns: bfloat16 [128, 131072], P('tm'), may hold values from -6 to 6
- start: int32 [1], replicated, may hold values from 0 to 131056
- exposures: bfloat16 [512, 131072], P('acct', 'tm'), may hold values from -0.125 to 0.125
- links: int32 [512], replicated, may hold values from 0 to 127
Outputs:
- cov_block: bfloat16 [16, 131072], P('acct', 'tm')
- house_totals: float32 [16, 128], replicated
The draws below stay inside these ranges and needn't reach their ends.
All inputs are finite; a program needn't handle non-finite values.
Results may differ from the reference program's by a relative error of at most 0.005.
Values may be sent and summed in bfloat16 or wider, within the bound.
A program may use at most 64 MiB of HBM per device.

```python
import math
import jax
import jax.numpy as jnp
from jax import lax

F = 131072
HOUSES = 128
DAYS = 128
B = 16
A = 512


def plant(values, own_key, least, largest):
    dims = values.shape
    spot = [jax.random.randint(jax.random.fold_in(own_key, axis), (), 0, dims[axis]) for axis in range(len(dims))]
    values = values.at[tuple(spot)].set(least)
    longest = dims.index(max(dims))
    spot[longest] = (spot[longest] + 1) % dims[longest]
    return values.at[tuple(spot)].set(largest)


def levels(stream_key, dims, pieces, low, high):
    factor_of = 1.0
    for axis_at, shards_of in pieces:
        draws = jax.random.uniform(jax.random.fold_in(jax.random.fold_in(stream_key, 6), axis_at), (shards_of,), jnp.float32, low / len(pieces), high / len(pieces))
        factor_of = factor_of * jnp.repeat(jnp.exp(draws), dims[axis_at] // shards_of).reshape((-1,) + (1,) * (len(dims) - 1 - axis_at))
    return factor_of


def scatter_about(own_key, extent, deviation, most, shards=(), held_as=jnp.bfloat16):
    factor_of = levels(own_key, extent, shards, -0.22, 0.18) if shards else 1.0
    entries = jax.random.normal(own_key, extent, jnp.float32) * deviation * factor_of
    return jnp.minimum(jnp.maximum(entries, -most), most).astype(held_as)


def setup_inputs(seed: int = 0) -> dict:
    key_list = jax.random.split(jax.random.key(seed), 5)
    return {
        "returns": scatter_about(key_list[0], (DAYS, F), 1.0, 6.0, ((0, 16),)),
        "start": jax.random.randint(key_list[1], (1,), 0, F - B + 1).astype(jnp.int32),
        "exposures": scatter_about(key_list[2], (A, F), (F // 64) ** -0.5, 0.125, ((0, 2), (1, 16))),
        "links": plant(jax.random.randint(key_list[3], (A,), 0, HOUSES), jax.random.fold_in(key_list[3], 1), 0, HOUSES - 1).astype(jnp.int32),
    }


def day_weights(total_days):
    days = jnp.arange(total_days, dtype=jnp.float32)
    raw = jnp.exp(-math.log(3.0) * (total_days - 1.0 - days) / total_days)
    return raw / jnp.sum(raw)


def reference(returns, start, exposures, links):
    weights = day_weights(returns.shape[0])
    rows = lax.dynamic_slice_in_dim(returns, start[0].astype(jnp.int32), B, 1)
    block = (rows.astype(jnp.float32) * weights[:, None]).astype(jnp.bfloat16)
    cov_block = lax.dot_general(block, returns, (((0,), (0,)), ((), ())), preferred_element_type=jnp.float32).astype(jnp.bfloat16)
    loads = lax.dot_general(cov_block, exposures, (((1,), (1,)), ((), ())), preferred_element_type=jnp.float32)
    onehot = (links[:, None] == jnp.arange(HOUSES, dtype=jnp.int32)[None, :]).astype(jnp.float32)
    house_totals = jnp.dot(loads, onehot, precision=lax.Precision.HIGHEST)
    return cov_block, house_totals
```

```python
import functools
import math

import jax
import jax.numpy as jnp
from jax import lax
from jax.experimental import pallas as pl
from jax.experimental.pallas import tpu as pltpu
from jax.sharding import PartitionSpec as P

HOUSES = 128
LANES = 128
MESH = pl.DeviceIdType.MESH


def least_divisor(count):
    return min((d for d in range(2, count + 1) if count % d == 0), default=1)


def flip(value, mask):
    bit = 1
    while bit <= mask:
        if mask & bit:
            value = value + bit * (1 - 2 * lax.rem(value // bit, 2))
        bit *= 2
    return value


def kernel(
    sizes,
    start_ref, links_ref, tiles_hbm, returns_hbm, exposures_hbm,
    cov_hbm, totals_ref,
    tiles, exps, gathered, blocks, turned, sent, received, covs, slots1, slots2,
    local_sem, own_sem, dsend, drecv, bsend, brecv, zsend, zrecv, fsend, frecv,
    send1, recv1, send2, recv2,
):
    tms, accts, low, near, parts, rows_dev = sizes
    days, factors = returns_hbm.shape
    depth = tms // near
    all_days = days * tms
    rows = rows_dev * accts
    cols = factors // tms
    piece = cols // accts
    own_accounts = exps.shape[0]
    me, acct = lax.axis_index("tm"), lax.axis_index("acct")
    place, layer = lax.rem(me, low), me // low
    member, level = lax.rem(me, near), me // near

    def at_acct(shift):
        return lax.rem(acct + shift, accts)

    def peer(mask):
        return level * near + flip(member, mask)

    def above(mask):
        return flip(level, mask) * near + member

    def span_of(owner, at, size):
        return pl.ds(pl.multiple_of(owner * cols + acct * piece + at, LANES), size)

    masks = range(1, near)
    hops = [1 << bit for bit in range(depth.bit_length() - 1)]
    load_tiles = pltpu.make_async_copy(tiles_hbm, tiles, local_sem.at[2])
    load_tiles.start()
    loads_own = []
    for r in reversed(range(depth)):
        owner = flip(level, r) * near + member
        copy = pltpu.make_async_copy(
            returns_hbm.at[:, span_of(owner, 0, piece)], gathered.at[member, r], own_sem.at[r]
        )
        copy.start()
        loads_own.append(copy)

    barrier = pltpu.get_barrier_semaphore()
    greeted = 0
    for mask in masks:
        pl.semaphore_signal(barrier, inc=1, device_id=(peer(mask), acct), device_id_type=MESH)
        greeted += 1
    for hop in hops:
        pl.semaphore_signal(barrier, inc=1, device_id=(above(hop), acct), device_id_type=MESH)
        greeted += 1
    for step in range(low):
        for hop in range(1, accts):
            other = layer * low + lax.rem(place + step, low)
            pl.semaphore_signal(barrier, inc=1, device_id=(other, at_acct(hop)), device_id_type=MESH)
            greeted += 1
    load_exps = pltpu.make_async_copy(exposures_hbm, exps, local_sem.at[1])
    load_exps.start()
    pl.semaphore_wait(barrier, greeted)

    chunks = [(r, index) for r in reversed(range(depth)) for index in range(len(parts))]
    order = [mask for mask in masks if mask >= low] + [mask for mask in masks if mask < low]
    sends = []

    def raw(r, index, mask, source):
        at, size = parts[index]
        owner = flip(level, r) * near + flip(member, mask)
        return pltpu.make_async_remote_copy(
            src_ref=returns_hbm.at[:, span_of(owner, at, size)],
            dst_ref=gathered.at[source, r, :, pl.ds(at, size)],
            send_sem=dsend.at[r, index, mask], recv_sem=drecv.at[r, index, mask],
            device_id=(peer(mask), acct), device_id_type=MESH,
        )

    def start_raw(r, index):
        for mask in order:
            copy = raw(r, index, mask, member)
            copy.start()
            sends.append(copy)

    start_raw(*chunks[0])

    load_tiles.wait()
    tile_count = tiles.shape[0]
    first_tile = lax.div(start_ref[0], LANES)
    window = jnp.concatenate(
        [tiles[first_tile], tiles[jnp.minimum(first_tile + 1, tile_count - 1)]], axis=1
    )
    offset = start_ref[0] - first_tile * LANES
    source = lax.broadcasted_iota(jnp.int32, (2 * LANES, LANES), 0)
    target = lax.broadcasted_iota(jnp.int32, (2 * LANES, LANES), 1)
    pick = jnp.where((source == target + offset) & (target < rows), 1.0, 0.0)
    picked = jnp.dot(window, pick.astype(jnp.bfloat16), preferred_element_type=jnp.float32)

    def raw_weight(day):
        return jnp.exp(-math.log(3.0) * (all_days - 1.0 - day.astype(jnp.float32)) / all_days)

    total = jnp.sum(
        raw_weight(lax.broadcasted_iota(jnp.int32, (days, all_days), 1)), axis=1, keepdims=True
    )
    weights = raw_weight(me * days + lax.broadcasted_iota(jnp.int32, (days, LANES), 0)) / total
    blocks[member] = (picked * weights).astype(jnp.bfloat16)

    def block_copy(mask, slot):
        return pltpu.make_async_remote_copy(
            src_ref=blocks.at[slot], dst_ref=blocks.at[slot],
            send_sem=bsend.at[mask], recv_sem=brecv.at[mask],
            device_id=(peer(mask), acct), device_id_type=MESH,
        )

    for mask in order:
        copy = block_copy(mask, member)
        copy.start()
        sends.append(copy)
    for chunk in chunks[1:]:
        start_raw(*chunk)

    for mask in masks:
        block_copy(mask, flip(member, mask)).wait_recv()
    turned[...] = blocks[...].astype(jnp.float32).reshape(days * near, LANES).T
    left = turned[:rows, :].astype(jnp.bfloat16)

    def columns(owner, at, size):
        return pl.ds(pl.multiple_of(owner * piece + at, LANES), size)

    def exchange(index, hop, owner):
        held = covs.at[:, :, columns(owner, *parts[index])]
        return pltpu.make_async_remote_copy(
            src_ref=held, dst_ref=held,
            send_sem=fsend.at[index, hop], recv_sem=frecv.at[index, hop],
            device_id=(me, at_acct(hop)), device_id_type=MESH,
        )

    def loads_of(owner, index):
        span = columns(owner, *parts[index])
        cov = covs[:, :, span].astype(jnp.float32).reshape(rows, parts[index][1])
        return lax.dot_general(
            cov.astype(jnp.bfloat16), exps[:, span], (((1,), (1,)), ((), ())),
            preferred_element_type=jnp.float32,
        )

    def partial(r, index):
        at, size = parts[index]
        held = pl.ds(at, size)
        hop = r & -r
        return pltpu.make_async_remote_copy(
            src_ref=sent.at[r - 1, :, held], dst_ref=received.at[r - 1, :, held],
            send_sem=zsend.at[r, index], recv_sem=zrecv.at[r, index],
            device_id=(above(hop), acct), device_id_type=MESH,
        )

    for r, index in chunks:
        first, size = parts[index]
        if index == 0:
            loads_own[depth - 1 - r].wait()
        for mask in masks:
            raw(r, index, mask, flip(member, mask)).wait_recv()
        arrivals = [r + hop for hop in hops if r == 0 or hop < (r & -r)]
        for arrival in reversed(arrivals):
            partial(arrival, index).wait_recv()
        width = math.gcd(size, 1024)
        for at in range(first, first + size, width):
            tile = gathered[:, r, :, pl.ds(at, width)].astype(jnp.float32)
            cov = jnp.dot(
                left, tile.reshape(days * near, width).astype(jnp.bfloat16),
                preferred_element_type=jnp.float32,
            )
            for arrival in arrivals:
                cov += received[arrival - 1, :, pl.ds(at, width)].astype(jnp.float32)
            if r:
                sent[r - 1, :, pl.ds(at, width)] = cov.astype(jnp.bfloat16)
            else:
                covs[:, :, columns(acct, at, width)] = cov.reshape(accts, rows_dev, width).astype(
                    jnp.bfloat16
                )
        if r:
            copy = partial(r, index)
            copy.start()
            sends.append(copy)
        else:
            for hop in range(1, accts):
                copy = exchange(index, hop, acct)
                copy.start()
                sends.append(copy)

    load_exps.wait()
    loads = jnp.zeros((rows, own_accounts), jnp.float32)
    for index in range(len(parts)):
        loads += loads_of(acct, index)
    for index in range(len(parts)):
        for hop in range(1, accts):
            owner = at_acct(accts - hop)
            exchange(index, hop, owner).wait_recv()
            loads += loads_of(owner, index)
    store_cov = pltpu.make_async_copy(covs.at[acct], cov_hbm, local_sem.at[0])
    store_cov.start()

    links = links_ref[:, pl.ds(pl.multiple_of(acct * own_accounts, LANES), own_accounts)]
    house = lax.broadcasted_iota(jnp.int32, (HOUSES, own_accounts), 0)
    in_house = jnp.where(house == links, 1.0, 0.0)
    mine = place * accts + acct
    slots1[mine] = lax.dot_general(
        loads, in_house, (((1,), (1,)), ((), ())),
        precision=lax.Precision.HIGHEST, preferred_element_type=jnp.float32,
    )

    group = low * accts
    for step in range(1, group):
        other = layer * low + lax.rem(place + step // accts, low)
        copy = pltpu.make_async_remote_copy(
            src_ref=slots1.at[mine], dst_ref=slots1.at[mine],
            send_sem=send1.at[step], recv_sem=recv1.at[step],
            device_id=(other, at_acct(step % accts)), device_id_type=MESH,
        )
        copy.start()
        sends.append(copy)
    for step in range(1, group):
        sender = lax.rem(place + low - step // accts, low) * accts + at_acct(accts - step % accts)
        pltpu.make_async_remote_copy(
            src_ref=slots1.at[sender], dst_ref=slots1.at[sender],
            send_sem=send1.at[step], recv_sem=recv1.at[step],
            device_id=(me, at_acct(accts - 1)), device_id_type=MESH,
        ).wait_recv()
    slots2[layer] = jnp.sum(slots1[...], axis=0)
    layers = tms // low
    for step in range(1, layers):
        copy = pltpu.make_async_remote_copy(
            src_ref=slots2.at[layer], dst_ref=slots2.at[layer],
            send_sem=send2.at[step], recv_sem=recv2.at[step],
            device_id=(lax.rem(layer + step, layers) * low + place, acct), device_id_type=MESH,
        )
        copy.start()
        sends.append(copy)
    for step in range(1, layers):
        sender = lax.rem(layer + layers - step, layers)
        pltpu.make_async_remote_copy(
            src_ref=slots2.at[sender], dst_ref=slots2.at[sender],
            send_sem=send2.at[step], recv_sem=recv2.at[step],
            device_id=(me, at_acct(accts - 1)), device_id_type=MESH,
        ).wait_recv()
    totals_ref[...] = jnp.sum(slots2[...], axis=0)
    for copy in sends:
        copy.wait_send()
    store_cov.wait()


def hand_over(cov_ref, totals_ref, cov_out, totals_out):
    cov_out[...] = cov_ref[...]
    totals_out[...] = totals_ref[...]


def on_device(tms, accts, returns, start, exposures, links):
    days, factors = returns.shape
    own_accounts, cols = exposures.shape
    rows_dev = 8
    rows = rows_dev * accts
    low = least_divisor(tms)
    near = low * least_divisor(tms // low)
    depth = tms // near
    piece = cols // accts
    last = max(LANES, piece // 2 // LANES * LANES)
    parts = [(at, size) for at, size in ((0, piece - last), (piece - last, last)) if size]
    tiles = returns.reshape(days, factors // LANES, LANES).transpose(1, 0, 2)
    dma = pltpu.SemaphoreType.DMA
    count = len(parts)
    cov, totals = pl.pallas_call(
        functools.partial(kernel, (tms, accts, low, near, parts, rows_dev)),
        out_shape=(
            jax.ShapeDtypeStruct((rows_dev, cols), jnp.bfloat16),
            jax.ShapeDtypeStruct((rows, HOUSES), jnp.float32),
        ),
        in_specs=[
            pl.BlockSpec(memory_space=pltpu.SMEM),
            pl.BlockSpec(memory_space=pltpu.VMEM),
            pl.BlockSpec(memory_space=pl.ANY),
            pl.BlockSpec(memory_space=pl.ANY),
            pl.BlockSpec(memory_space=pl.ANY),
        ],
        out_specs=(
            pl.BlockSpec(memory_space=pl.ANY),
            pl.BlockSpec(memory_space=pltpu.VMEM),
        ),
        scratch_shapes=[
            pltpu.VMEM((factors // LANES, days, LANES), returns.dtype),
            pltpu.VMEM((own_accounts, cols), exposures.dtype),
            pltpu.VMEM((near, depth, days, piece), returns.dtype),
            pltpu.VMEM((near, days, LANES), jnp.bfloat16),
            pltpu.VMEM((LANES, days * near), jnp.float32),
            pltpu.VMEM((max(depth - 1, 1), rows, piece), jnp.bfloat16),
            pltpu.VMEM((max(depth - 1, 1), rows, piece), jnp.bfloat16),
            pltpu.VMEM((accts, rows_dev, cols), jnp.bfloat16),
            pltpu.VMEM((low * accts, rows, HOUSES), jnp.float32),
            pltpu.VMEM((tms // low, rows, HOUSES), jnp.float32),
            dma((3,)), dma((depth,)),
            dma((depth, count, near)), dma((depth, count, near)), dma((near,)), dma((near,)),
            dma((depth, count)), dma((depth, count)),
            dma((count, accts)), dma((count, accts)),
            dma((low * accts,)), dma((low * accts,)),
            dma((tms // low,)), dma((tms // low,)),
        ],
        compiler_params=pltpu.CompilerParams(collective_id=0, has_side_effects=True),
        name="exposures_by_house",
    )(start, links[None, :], tiles, returns, exposures)
    return pl.pallas_call(
        hand_over,
        out_shape=(
            jax.ShapeDtypeStruct(cov.shape, cov.dtype),
            jax.ShapeDtypeStruct(totals.shape, totals.dtype),
        ),
        in_specs=[pl.BlockSpec(memory_space=pltpu.VMEM)] * 2,
        out_specs=(pl.BlockSpec(memory_space=pltpu.VMEM),) * 2,
        name="hand_over",
    )(cov, totals)


def solution(mesh):
    return jax.shard_map(
        functools.partial(on_device, mesh.shape["tm"], mesh.shape["acct"]),
        mesh=mesh,
        in_specs=(P("tm", None), P(), P("acct", "tm"), P()),
        out_specs=(P("acct", "tm"), P()),
        check_vma=False,
    )
```

```python
import functools
import math

import jax
import jax.numpy as jnp
from jax import lax
from jax.experimental import pallas as pl
from jax.experimental.pallas import tpu as pltpu
from jax.sharding import PartitionSpec as P

HOUSES = 128
LANES = 128
PARTS = 4
VMEM_LIMIT = 40 * 2**20
MESH = pl.DeviceIdType.MESH


def least_divisor(count):
    return min((d for d in range(2, count + 1) if count % d == 0), default=1)


def flip(value, mask):
    bit = 1
    while bit <= mask:
        if mask & bit:
            value = value + bit * (1 - 2 * lax.rem(value // bit, 2))
        bit *= 2
    return value


def kernel(
    sizes,
    start_ref, links_hbm, tiles_hbm, returns_hbm, exposures_hbm,
    cov_ref, totals_ref,
    links_ref, tiles, exps, by_house, gathered, blocks, turned, sent, received, covs, slots1, slots2,
    local_sem, own_sem, dsend, drecv, bsend, brecv, zsend, zrecv, fsend, frecv,
    send1, recv1, send2, recv2,
):
    tms, accts, low, near, parts, rows_dev = sizes
    days, factors = returns_hbm.shape
    depth = tms // near
    all_days = days * tms
    rows = rows_dev * accts
    cols = factors // tms
    piece = cols // accts
    own_accounts = exps.shape[0]
    me, acct = lax.axis_index("tm"), lax.axis_index("acct")
    place, layer = lax.rem(me, low), me // low
    member, level = lax.rem(me, near), me // near

    def at_acct(shift):
        return lax.rem(acct + shift, accts)

    def peer(mask):
        return level * near + flip(member, mask)

    def above(mask):
        return flip(level, mask) * near + member

    def span_of(owner, at, size):
        return pl.ds(pl.multiple_of(owner * cols + acct * piece + at, LANES), size)

    masks = range(1, near)
    hops = [1 << bit for bit in range(depth.bit_length() - 1)]
    barrier = pltpu.get_barrier_semaphore()
    greeted = 0
    for mask in masks:
        pl.semaphore_signal(barrier, inc=1, device_id=(peer(mask), acct), device_id_type=MESH)
        greeted += 1
    for hop in hops:
        pl.semaphore_signal(barrier, inc=1, device_id=(above(hop), acct), device_id_type=MESH)
        greeted += 1
    for step in range(low):
        for hop in range(1, accts):
            other = layer * low + lax.rem(place + step, low)
            pl.semaphore_signal(barrier, inc=1, device_id=(other, at_acct(hop)), device_id_type=MESH)
            greeted += 1
    load_tiles = pltpu.make_async_copy(tiles_hbm, tiles, local_sem.at[2])
    load_tiles.start()
    loads_own = []
    for r in reversed(range(depth)):
        owner = flip(level, r) * near + member
        copy = pltpu.make_async_copy(
            returns_hbm.at[:, span_of(owner, 0, piece)], gathered.at[member, r], own_sem.at[r]
        )
        copy.start()
        loads_own.append(copy)
    load_links = pltpu.make_async_copy(links_hbm, links_ref, local_sem.at[0])
    load_links.start()
    load_exps = pltpu.make_async_copy(exposures_hbm, exps, local_sem.at[1])
    load_exps.start()
    pl.semaphore_wait(barrier, greeted)

    chunks = [(r, index) for r in reversed(range(depth)) for index in range(len(parts))]
    order = [mask for mask in masks if mask >= low] + [mask for mask in masks if mask < low]
    sends = []

    def raw(r, index, mask, source):
        at, size = parts[index]
        owner = flip(level, r) * near + flip(member, mask)
        return pltpu.make_async_remote_copy(
            src_ref=returns_hbm.at[:, span_of(owner, at, size)],
            dst_ref=gathered.at[source, r, :, pl.ds(at, size)],
            send_sem=dsend.at[r, index, mask], recv_sem=drecv.at[r, index, mask],
            device_id=(peer(mask), acct), device_id_type=MESH,
        )

    def start_raw(r, index):
        for mask in order:
            copy = raw(r, index, mask, member)
            copy.start()
            sends.append(copy)

    start_raw(*chunks[0])

    load_tiles.wait()
    tile_count = tiles.shape[0]
    first_tile = lax.div(start_ref[0], LANES)
    window = jnp.concatenate(
        [tiles[first_tile], tiles[jnp.minimum(first_tile + 1, tile_count - 1)]], axis=1
    )
    offset = start_ref[0] - first_tile * LANES
    source = lax.broadcasted_iota(jnp.int32, (2 * LANES, LANES), 0)
    target = lax.broadcasted_iota(jnp.int32, (2 * LANES, LANES), 1)
    pick = jnp.where((source == target + offset) & (target < rows), 1.0, 0.0)
    picked = jnp.dot(window, pick.astype(jnp.bfloat16), preferred_element_type=jnp.float32)

    def raw_weight(day):
        return jnp.exp(-math.log(3.0) * (all_days - 1.0 - day.astype(jnp.float32)) / all_days)

    total = jnp.sum(
        raw_weight(lax.broadcasted_iota(jnp.int32, (days, all_days), 1)), axis=1, keepdims=True
    )
    weights = raw_weight(me * days + lax.broadcasted_iota(jnp.int32, (days, LANES), 0)) / total
    blocks[member] = (picked * weights).astype(jnp.bfloat16)

    def block_copy(mask, slot):
        return pltpu.make_async_remote_copy(
            src_ref=blocks.at[slot], dst_ref=blocks.at[slot],
            send_sem=bsend.at[mask], recv_sem=brecv.at[mask],
            device_id=(peer(mask), acct), device_id_type=MESH,
        )

    for mask in order:
        copy = block_copy(mask, member)
        copy.start()
        sends.append(copy)
    for chunk in chunks[1:]:
        start_raw(*chunk)

    for mask in masks:
        block_copy(mask, flip(member, mask)).wait_recv()
    turned[...] = blocks[...].astype(jnp.float32).reshape(days * near, LANES).T
    left = turned[:rows, :].astype(jnp.bfloat16)

    def columns(owner, at, size):
        return pl.ds(pl.multiple_of(owner * piece + at, LANES), size)

    def exchange(index, hop, owner):
        held = covs.at[:, :, columns(owner, *parts[index])]
        return pltpu.make_async_remote_copy(
            src_ref=held, dst_ref=held,
            send_sem=fsend.at[index, hop], recv_sem=frecv.at[index, hop],
            device_id=(me, at_acct(hop)), device_id_type=MESH,
        )

    load_links.wait()
    load_exps.wait()
    links = links_ref[:, pl.ds(pl.multiple_of(acct * own_accounts, LANES), own_accounts)]
    house = lax.broadcasted_iota(jnp.int32, (HOUSES, own_accounts), 0)
    in_house = jnp.where(house == links, 1.0, 0.0).astype(jnp.bfloat16)
    unit = math.gcd(cols, 512)
    units = cols // unit

    def sum_houses(first, last):
        for at in range(first * unit, last * unit, unit):
            held = pl.ds(at, unit)
            summed = jnp.dot(in_house, exps[:, held], preferred_element_type=jnp.float32)
            high = summed.astype(jnp.bfloat16)
            by_house[:HOUSES, held] = high
            by_house[HOUSES:, held] = (summed - high.astype(jnp.float32)).astype(jnp.bfloat16)

    def loads_of(owner, index):
        span = columns(owner, *parts[index])
        cov = covs[:, :, span].astype(jnp.float32).reshape(rows, parts[index][1])
        return lax.dot_general(
            cov.astype(jnp.bfloat16), by_house[:, span], (((1,), (1,)), ((), ())),
            preferred_element_type=jnp.float32,
        )

    def partial(r, index):
        at, size = parts[index]
        held = pl.ds(at, size)
        hop = r & -r
        return pltpu.make_async_remote_copy(
            src_ref=sent.at[r - 1, :, held], dst_ref=received.at[r - 1, :, held],
            send_sem=zsend.at[r, index], recv_sem=zrecv.at[r, index],
            device_id=(above(hop), acct), device_id_type=MESH,
        )

    loads = jnp.zeros((rows, 2 * HOUSES), jnp.float32)
    early = (depth - 1) * len(parts)
    for count, (r, index) in enumerate(chunks):
        first, size = parts[index]
        if index == 0:
            loads_own[depth - 1 - r].wait()
        for mask in masks:
            raw(r, index, mask, flip(member, mask)).wait_recv()
        arrivals = [r + hop for hop in hops if r == 0 or hop < (r & -r)]
        for arrival in reversed(arrivals):
            partial(arrival, index).wait_recv()
        width = math.gcd(size, 1024)
        for at in range(first, first + size, width):
            tile = gathered[:, r, :, pl.ds(at, width)].astype(jnp.float32)
            cov = jnp.dot(
                left, tile.reshape(days * near, width).astype(jnp.bfloat16),
                preferred_element_type=jnp.float32,
            )
            for arrival in arrivals:
                cov += received[arrival - 1, :, pl.ds(at, width)].astype(jnp.float32)
            if r:
                sent[r - 1, :, pl.ds(at, width)] = cov.astype(jnp.bfloat16)
            else:
                covs[:, :, columns(acct, at, width)] = cov.reshape(accts, rows_dev, width).astype(
                    jnp.bfloat16
                )
        if r:
            copy = partial(r, index)
            copy.start()
            sends.append(copy)
            sum_houses(units * count // early, units * (count + 1) // early)
        else:
            for hop in range(1, accts):
                copy = exchange(index, hop, acct)
                copy.start()
                sends.append(copy)
            loads += loads_of(acct, index)
    for index in range(len(parts)):
        for hop in range(1, accts):
            owner = at_acct(accts - hop)
            exchange(index, hop, owner).wait_recv()
            loads += loads_of(owner, index)
    mine = place * accts + acct
    slots1[mine] = loads[:, :HOUSES] + loads[:, HOUSES:]

    group = low * accts
    for step in range(1, group):
        other = layer * low + lax.rem(place + step // accts, low)
        copy = pltpu.make_async_remote_copy(
            src_ref=slots1.at[mine], dst_ref=slots1.at[mine],
            send_sem=send1.at[step], recv_sem=recv1.at[step],
            device_id=(other, at_acct(step % accts)), device_id_type=MESH,
        )
        copy.start()
        sends.append(copy)
    cov_ref[...] = covs[acct]
    for step in range(1, group):
        sender = lax.rem(place + low - step // accts, low) * accts + at_acct(accts - step % accts)
        pltpu.make_async_remote_copy(
            src_ref=slots1.at[sender], dst_ref=slots1.at[sender],
            send_sem=send1.at[step], recv_sem=recv1.at[step],
            device_id=(me, at_acct(accts - 1)), device_id_type=MESH,
        ).wait_recv()
    slots2[layer] = jnp.sum(slots1[...], axis=0)
    layers = tms // low
    for step in range(1, layers):
        copy = pltpu.make_async_remote_copy(
            src_ref=slots2.at[layer], dst_ref=slots2.at[layer],
            send_sem=send2.at[step], recv_sem=recv2.at[step],
            device_id=(lax.rem(layer + step, layers) * low + place, acct), device_id_type=MESH,
        )
        copy.start()
        sends.append(copy)
    for step in range(1, layers):
        sender = lax.rem(layer + layers - step, layers)
        pltpu.make_async_remote_copy(
            src_ref=slots2.at[sender], dst_ref=slots2.at[sender],
            send_sem=send2.at[step], recv_sem=recv2.at[step],
            device_id=(me, at_acct(accts - 1)), device_id_type=MESH,
        ).wait_recv()
    totals_ref[...] = jnp.sum(slots2[...], axis=0)
    for copy in sends:
        copy.wait_send()


def hand_over(cov_ref, totals_ref, cov_out, totals_out):
    cov_out[...] = cov_ref[...]
    totals_out[...] = totals_ref[...]


def on_device(tms, accts, returns, start, exposures, links):
    days, factors = returns.shape
    own_accounts, cols = exposures.shape
    rows_dev = 8
    rows = rows_dev * accts
    low = least_divisor(tms)
    near = low * least_divisor(tms // low)
    depth = tms // near
    piece = cols // accts
    width = max(LANES, piece // PARTS // LANES * LANES)
    parts = [(at, min(width, piece - at)) for at in range(0, piece, width)]
    tiles = returns.reshape(days, factors // LANES, LANES).transpose(1, 0, 2)
    held = functools.partial(pltpu.with_memory_space_constraint, memory_space=pltpu.HBM)
    dma = pltpu.SemaphoreType.DMA
    count = len(parts)
    cov, totals = pl.pallas_call(
        functools.partial(kernel, (tms, accts, low, near, parts, rows_dev)),
        out_shape=(
            jax.ShapeDtypeStruct((rows_dev, cols), jnp.bfloat16),
            jax.ShapeDtypeStruct((rows, HOUSES), jnp.float32),
        ),
        in_specs=[
            pl.BlockSpec(memory_space=pltpu.SMEM),
            pl.BlockSpec(memory_space=pl.ANY),
            pl.BlockSpec(memory_space=pl.ANY),
            pl.BlockSpec(memory_space=pl.ANY),
            pl.BlockSpec(memory_space=pl.ANY),
        ],
        out_specs=(pl.BlockSpec(memory_space=pltpu.VMEM),) * 2,
        scratch_shapes=[
            pltpu.VMEM((1, links.size), jnp.int32),
            pltpu.VMEM((factors // LANES, days, LANES), returns.dtype),
            pltpu.VMEM((own_accounts, cols), exposures.dtype),
            pltpu.VMEM((2 * HOUSES, cols), jnp.bfloat16),
            pltpu.VMEM((near, depth, days, piece), returns.dtype),
            pltpu.VMEM((near, days, LANES), jnp.bfloat16),
            pltpu.VMEM((LANES, days * near), jnp.float32),
            pltpu.VMEM((max(depth - 1, 1), rows, piece), jnp.bfloat16),
            pltpu.VMEM((max(depth - 1, 1), rows, piece), jnp.bfloat16),
            pltpu.VMEM((accts, rows_dev, cols), jnp.bfloat16),
            pltpu.VMEM((low * accts, rows, HOUSES), jnp.float32),
            pltpu.VMEM((tms // low, rows, HOUSES), jnp.float32),
            dma((3,)), dma((depth,)),
            dma((depth, count, near)), dma((depth, count, near)), dma((near,)), dma((near,)),
            dma((depth, count)), dma((depth, count)),
            dma((count, accts)), dma((count, accts)),
            dma((low * accts,)), dma((low * accts,)),
            dma((tms // low,)), dma((tms // low,)),
        ],
        compiler_params=pltpu.CompilerParams(
            collective_id=0, has_side_effects=True, vmem_limit_bytes=VMEM_LIMIT
        ),
        name="exposures_by_house",
    )(start, *(held(array) for array in (links[None, :], tiles, returns, exposures)))
    return pl.pallas_call(
        hand_over,
        out_shape=(
            jax.ShapeDtypeStruct(cov.shape, cov.dtype),
            jax.ShapeDtypeStruct(totals.shape, totals.dtype),
        ),
        in_specs=[pl.BlockSpec(memory_space=pltpu.VMEM)] * 2,
        out_specs=(pl.BlockSpec(memory_space=pltpu.VMEM),) * 2,
        compiler_params=pltpu.CompilerParams(vmem_limit_bytes=VMEM_LIMIT),
        name="hand_over",
    )(cov, totals)


def solution(mesh):
    return jax.shard_map(
        functools.partial(on_device, mesh.shape["tm"], mesh.shape["acct"]),
        mesh=mesh,
        in_specs=(P("tm", None), P(), P("acct", "tm"), P()),
        out_specs=(P("acct", "tm"), P()),
        check_vma=False,
    )
```

```python
import functools
import math

import jax
import jax.numpy as jnp
from jax import lax
from jax.experimental import pallas as pl
from jax.experimental.pallas import tpu as pltpu
from jax.sharding import PartitionSpec as P

HOUSES = 128
LANES = 128
PARTS = 2
VMEM_LIMIT = 40 * 2**20
MESH = pl.DeviceIdType.MESH


def least_divisor(count):
    return min((d for d in range(2, count + 1) if count % d == 0), default=1)


def flip(value, mask):
    bit = 1
    while bit <= mask:
        if mask & bit:
            value = value + bit * (1 - 2 * lax.rem(value // bit, 2))
        bit *= 2
    return value


def kernel(
    sizes,
    start_ref, links_hbm, tiles_hbm, returns_hbm, exposures_hbm,
    cov_ref, totals_ref,
    links_ref, tiles, exps, by_house, gathered, blocks, turned, sent, received, covs, slots1, slots2,
    local_sem, own_sem, dsend, drecv, bsend, brecv, zsend, zrecv, fsend, frecv,
    send1, recv1, send2, recv2,
):
    tms, accts, low, near, parts, rows_dev = sizes
    days, factors = returns_hbm.shape
    depth = tms // near
    all_days = days * tms
    rows = rows_dev * accts
    cols = factors // tms
    piece = cols // accts
    own_accounts = exps.shape[0]
    me, acct = lax.axis_index("tm"), lax.axis_index("acct")
    place, layer = lax.rem(me, low), me // low
    member, level = lax.rem(me, near), me // near

    def at_acct(shift):
        return lax.rem(acct + shift, accts)

    def peer(mask):
        return level * near + flip(member, mask)

    def above(mask):
        return flip(level, mask) * near + member

    def span_of(owner, at, size):
        return pl.ds(pl.multiple_of(owner * cols + acct * piece + at, LANES), size)

    masks = range(1, near)
    hops = [1 << bit for bit in range(depth.bit_length() - 1)]
    barrier = pltpu.get_barrier_semaphore()
    greeted = 0
    for mask in masks:
        pl.semaphore_signal(barrier, inc=1, device_id=(peer(mask), acct), device_id_type=MESH)
        greeted += 1
    for hop in hops:
        pl.semaphore_signal(barrier, inc=1, device_id=(above(hop), acct), device_id_type=MESH)
        greeted += 1
    for step in range(low):
        for hop in range(1, accts):
            other = layer * low + lax.rem(place + step, low)
            pl.semaphore_signal(barrier, inc=1, device_id=(other, at_acct(hop)), device_id_type=MESH)
            greeted += 1
    load_tiles = pltpu.make_async_copy(tiles_hbm, tiles, local_sem.at[2])
    load_tiles.start()
    loads_own = []
    for r in reversed(range(depth)):
        owner = flip(level, r) * near + member
        copy = pltpu.make_async_copy(
            returns_hbm.at[:, span_of(owner, 0, piece)], gathered.at[member, r], own_sem.at[r]
        )
        copy.start()
        loads_own.append(copy)
    load_links = pltpu.make_async_copy(links_hbm, links_ref, local_sem.at[0])
    load_links.start()
    load_exps = pltpu.make_async_copy(exposures_hbm, exps, local_sem.at[1])
    load_exps.start()
    pl.semaphore_wait(barrier, greeted)

    chunks = [(r, index) for r in reversed(range(depth)) for index in range(len(parts))]
    order = [mask for mask in masks if mask >= low] + [mask for mask in masks if mask < low]
    sends = []

    def raw(r, index, mask, source):
        at, size = parts[index]
        owner = flip(level, r) * near + flip(member, mask)
        return pltpu.make_async_remote_copy(
            src_ref=returns_hbm.at[:, span_of(owner, at, size)],
            dst_ref=gathered.at[source, r, :, pl.ds(at, size)],
            send_sem=dsend.at[r, index, mask], recv_sem=drecv.at[r, index, mask],
            device_id=(peer(mask), acct), device_id_type=MESH,
        )

    def start_raw(r, index):
        for mask in order:
            copy = raw(r, index, mask, member)
            copy.start()
            sends.append(copy)

    start_raw(*chunks[0])

    load_tiles.wait()
    tile_count = tiles.shape[0]
    first_tile = lax.div(start_ref[0], LANES)
    window = jnp.concatenate(
        [tiles[first_tile], tiles[jnp.minimum(first_tile + 1, tile_count - 1)]], axis=1
    )
    offset = start_ref[0] - first_tile * LANES
    source = lax.broadcasted_iota(jnp.int32, (2 * LANES, LANES), 0)
    target = lax.broadcasted_iota(jnp.int32, (2 * LANES, LANES), 1)
    pick = jnp.where((source == target + offset) & (target < rows), 1.0, 0.0)
    picked = jnp.dot(window, pick.astype(jnp.bfloat16), preferred_element_type=jnp.float32)

    def raw_weight(day):
        return jnp.exp(-math.log(3.0) * (all_days - 1.0 - day.astype(jnp.float32)) / all_days)

    total = jnp.sum(
        raw_weight(lax.broadcasted_iota(jnp.int32, (days, all_days), 1)), axis=1, keepdims=True
    )
    weights = raw_weight(me * days + lax.broadcasted_iota(jnp.int32, (days, LANES), 0)) / total
    blocks[member] = (picked * weights).astype(jnp.bfloat16)

    def block_copy(mask, slot):
        return pltpu.make_async_remote_copy(
            src_ref=blocks.at[slot], dst_ref=blocks.at[slot],
            send_sem=bsend.at[mask], recv_sem=brecv.at[mask],
            device_id=(peer(mask), acct), device_id_type=MESH,
        )

    for mask in order:
        copy = block_copy(mask, member)
        copy.start()
        sends.append(copy)
    for chunk in chunks[1:]:
        start_raw(*chunk)

    for mask in masks:
        block_copy(mask, flip(member, mask)).wait_recv()
    turned[...] = blocks[...].astype(jnp.float32).reshape(days * near, LANES).T
    left = turned[:rows, :].astype(jnp.bfloat16)

    def columns(owner, at, size):
        return pl.ds(pl.multiple_of(owner * piece + at, LANES), size)

    def exchange(index, hop, owner):
        held = covs.at[:, :, columns(owner, *parts[index])]
        return pltpu.make_async_remote_copy(
            src_ref=held, dst_ref=held,
            send_sem=fsend.at[index, hop], recv_sem=frecv.at[index, hop],
            device_id=(me, at_acct(hop)), device_id_type=MESH,
        )

    load_links.wait()
    load_exps.wait()
    links = links_ref[:, pl.ds(pl.multiple_of(acct * own_accounts, LANES), own_accounts)]
    house = lax.broadcasted_iota(jnp.int32, (HOUSES, own_accounts), 0)
    in_house = jnp.where(house == links, 1.0, 0.0).astype(jnp.bfloat16)
    unit = math.gcd(cols, 512)
    units = cols // unit

    def sum_houses(first, last):
        for at in range(first * unit, last * unit, unit):
            held = pl.ds(at, unit)
            summed = jnp.dot(in_house, exps[:, held], preferred_element_type=jnp.float32)
            high = summed.astype(jnp.bfloat16)
            by_house[:HOUSES, held] = high
            by_house[HOUSES:, held] = (summed - high.astype(jnp.float32)).astype(jnp.bfloat16)

    def loads_of(owner, index):
        span = columns(owner, *parts[index])
        cov = covs[:, :, span].astype(jnp.float32).reshape(rows, parts[index][1])
        return lax.dot_general(
            cov.astype(jnp.bfloat16), by_house[:, span], (((1,), (1,)), ((), ())),
            preferred_element_type=jnp.float32,
        )

    def partial(r, index):
        at, size = parts[index]
        held = pl.ds(at, size)
        hop = r & -r
        return pltpu.make_async_remote_copy(
            src_ref=sent.at[r - 1, :, held], dst_ref=received.at[r - 1, :, held],
            send_sem=zsend.at[r, index], recv_sem=zrecv.at[r, index],
            device_id=(above(hop), acct), device_id_type=MESH,
        )

    loads = jnp.zeros((rows, 2 * HOUSES), jnp.float32)
    early = (depth - 1) * len(parts)
    for count, (r, index) in enumerate(chunks):
        first, size = parts[index]
        if index == 0:
            loads_own[depth - 1 - r].wait()
        for mask in masks:
            raw(r, index, mask, flip(member, mask)).wait_recv()
        arrivals = [r + hop for hop in hops if r == 0 or hop < (r & -r)]
        for arrival in reversed(arrivals):
            partial(arrival, index).wait_recv()
        width = math.gcd(size, 1024)
        for at in range(first, first + size, width):
            tile = gathered[:, r, :, pl.ds(at, width)].astype(jnp.float32)
            cov = jnp.dot(
                left, tile.reshape(days * near, width).astype(jnp.bfloat16),
                preferred_element_type=jnp.float32,
            )
            for arrival in arrivals:
                cov += received[arrival - 1, :, pl.ds(at, width)].astype(jnp.float32)
            if r:
                sent[r - 1, :, pl.ds(at, width)] = cov.astype(jnp.bfloat16)
            else:
                covs[:, :, columns(acct, at, width)] = cov.reshape(accts, rows_dev, width).astype(
                    jnp.bfloat16
                )
        if r:
            copy = partial(r, index)
            copy.start()
            sends.append(copy)
            sum_houses(units * count // early, units * (count + 1) // early)
        else:
            for hop in range(1, accts):
                copy = exchange(index, hop, acct)
                copy.start()
                sends.append(copy)
            loads += loads_of(acct, index)
    for index in range(len(parts)):
        for hop in range(1, accts):
            owner = at_acct(accts - hop)
            exchange(index, hop, owner).wait_recv()
            loads += loads_of(owner, index)
    mine = place * accts + acct
    slots1[mine] = loads[:, :HOUSES] + loads[:, HOUSES:]

    group = low * accts
    for step in range(1, group):
        other = layer * low + lax.rem(place + step // accts, low)
        copy = pltpu.make_async_remote_copy(
            src_ref=slots1.at[mine], dst_ref=slots1.at[mine],
            send_sem=send1.at[step], recv_sem=recv1.at[step],
            device_id=(other, at_acct(step % accts)), device_id_type=MESH,
        )
        copy.start()
        sends.append(copy)
    cov_ref[...] = covs[acct]
    for step in range(1, group):
        sender = lax.rem(place + low - step // accts, low) * accts + at_acct(accts - step % accts)
        pltpu.make_async_remote_copy(
            src_ref=slots1.at[sender], dst_ref=slots1.at[sender],
            send_sem=send1.at[step], recv_sem=recv1.at[step],
            device_id=(me, at_acct(accts - 1)), device_id_type=MESH,
        ).wait_recv()
    slots2[layer] = jnp.sum(slots1[...], axis=0)
    layers = tms // low
    for step in range(1, layers):
        copy = pltpu.make_async_remote_copy(
            src_ref=slots2.at[layer], dst_ref=slots2.at[layer],
            send_sem=send2.at[step], recv_sem=recv2.at[step],
            device_id=(lax.rem(layer + step, layers) * low + place, acct), device_id_type=MESH,
        )
        copy.start()
        sends.append(copy)
    for step in range(1, layers):
        sender = lax.rem(layer + layers - step, layers)
        pltpu.make_async_remote_copy(
            src_ref=slots2.at[sender], dst_ref=slots2.at[sender],
            send_sem=send2.at[step], recv_sem=recv2.at[step],
            device_id=(me, at_acct(accts - 1)), device_id_type=MESH,
        ).wait_recv()
    totals_ref[...] = jnp.sum(slots2[...], axis=0)
    for copy in sends:
        copy.wait_send()


def hand_over(cov_ref, totals_ref, cov_out, totals_out):
    cov_out[...] = cov_ref[...]
    totals_out[...] = totals_ref[...]


def on_device(tms, accts, returns, start, exposures, links):
    days, factors = returns.shape
    own_accounts, cols = exposures.shape
    rows_dev = 8
    rows = rows_dev * accts
    low = least_divisor(tms)
    near = low * least_divisor(tms // low)
    depth = tms // near
    piece = cols // accts
    width = max(LANES, piece // PARTS // LANES * LANES)
    parts = [(at, min(width, piece - at)) for at in range(0, piece, width)]
    tiles = returns.reshape(days, factors // LANES, LANES).transpose(1, 0, 2)
    held = functools.partial(pltpu.with_memory_space_constraint, memory_space=pltpu.HBM)
    dma = pltpu.SemaphoreType.DMA
    count = len(parts)
    cov, totals = pl.pallas_call(
        functools.partial(kernel, (tms, accts, low, near, parts, rows_dev)),
        out_shape=(
            jax.ShapeDtypeStruct((rows_dev, cols), jnp.bfloat16),
            jax.ShapeDtypeStruct((rows, HOUSES), jnp.float32),
        ),
        in_specs=[
            pl.BlockSpec(memory_space=pltpu.SMEM),
            pl.BlockSpec(memory_space=pl.ANY),
            pl.BlockSpec(memory_space=pl.ANY),
            pl.BlockSpec(memory_space=pl.ANY),
            pl.BlockSpec(memory_space=pl.ANY),
        ],
        out_specs=(pl.BlockSpec(memory_space=pltpu.VMEM),) * 2,
        scratch_shapes=[
            pltpu.VMEM((1, links.size), jnp.int32),
            pltpu.VMEM((factors // LANES, days, LANES), returns.dtype),
            pltpu.VMEM((own_accounts, cols), exposures.dtype),
            pltpu.VMEM((2 * HOUSES, cols), jnp.bfloat16),
            pltpu.VMEM((near, depth, days, piece), returns.dtype),
            pltpu.VMEM((near, days, LANES), jnp.bfloat16),
            pltpu.VMEM((LANES, days * near), jnp.float32),
            pltpu.VMEM((max(depth - 1, 1), rows, piece), jnp.bfloat16),
            pltpu.VMEM((max(depth - 1, 1), rows, piece), jnp.bfloat16),
            pltpu.VMEM((accts, rows_dev, cols), jnp.bfloat16),
            pltpu.VMEM((low * accts, rows, HOUSES), jnp.float32),
            pltpu.VMEM((tms // low, rows, HOUSES), jnp.float32),
            dma((3,)), dma((depth,)),
            dma((depth, count, near)), dma((depth, count, near)), dma((near,)), dma((near,)),
            dma((depth, count)), dma((depth, count)),
            dma((count, accts)), dma((count, accts)),
            dma((low * accts,)), dma((low * accts,)),
            dma((tms // low,)), dma((tms // low,)),
        ],
        compiler_params=pltpu.CompilerParams(
            collective_id=0, has_side_effects=True, vmem_limit_bytes=VMEM_LIMIT
        ),
        name="exposures_by_house",
    )(start, *(held(array) for array in (links[None, :], tiles, returns, exposures)))
    return pl.pallas_call(
        hand_over,
        out_shape=(
            jax.ShapeDtypeStruct(cov.shape, cov.dtype),
            jax.ShapeDtypeStruct(totals.shape, totals.dtype),
        ),
        in_specs=[pl.BlockSpec(memory_space=pltpu.VMEM)] * 2,
        out_specs=(pl.BlockSpec(memory_space=pltpu.VMEM),) * 2,
        compiler_params=pltpu.CompilerParams(vmem_limit_bytes=VMEM_LIMIT),
        name="hand_over",
    )(cov, totals)


def solution(mesh):
    return jax.shard_map(
        functools.partial(on_device, mesh.shape["tm"], mesh.shape["acct"]),
        mesh=mesh,
        in_specs=(P("tm", None), P(), P("acct", "tm"), P()),
        out_specs=(P("acct", "tm"), P()),
        check_vma=False,
    )
```
